256 devices in a mesh: prow: 8 (over x_hi, y), pcol: 32 (over z, x_lo, core).
Axes of the slice: x: 4 (x_hi: 2, x_lo: 2; x = x_hi * 2 + x_lo), y: 4, z: 8, core: 2. Of those that a mesh axis runs over, the one named last changes fastest.
Arguments:
- trailing: float32 [8192, 8192], P('prow', 'pcol'), may hold values from -4 to 4
- anc_inverse: float32 [8192, 8192], P('prow', 'pcol'), as said below
- lower_panels: float32 [2, 8192, 1024], P(None, ('prow', 'pcol')), may hold values from -6 to 6
- upper_panels_t: float32 [2, 8192, 1024], P(None, 'pcol', 'prow'), may hold values from -0.078125 to 0.078125
- pivot_inverse: float32 [2, 1024, 1024], P(None, 'pcol'), as said below
- ancestors: int32 [2, 6], replicated, may hold values from 0 to 7, all different within a row
Outputs:
- schur: float32 [8192, 8192], P('prow', 'pcol')
- inverse_panels: float32 [2, 8192, 1024], P(None, 'pcol', 'prow')
- diag_inverse: float32 [2, 1024, 1024], P(None, 'pcol', 'prow')
The draws below stay inside these ranges and needn't reach their ends.
Inputs may be any that keep to these rules, and one draw needn't show every extreme that they name: anc_inverse is exactly symmetric and positive definite. Each pivot_inverse[k] is exactly symmetric and positive definite. `ancestors`: each row names 6 different ancestor blocks; every block of the window is named by some row.
All inputs are finite; a program needn't handle non-finite values.
Results may differ from the reference program's by a relative error of at most 0.0001.
Values sent between devices are 32-bit elements; how exact they have to be, the bound alone decides.
A program may use at most 128 MiB of HBM per device.

```python
import jax
import jax.numpy as jnp
from jax import lax

B = 1024
NB = 8
P_SIZE = 6
SUPERNODES = 2
NTOT = 8192


def symmetric_draw(key, order, diag_lo, diag_hi):
    first_key, second_key = jax.random.split(jax.random.fold_in(key, 17))
    entries = jax.random.normal(first_key, (order, order), jnp.float32)
    diagonal = jax.random.uniform(second_key, (order,), jnp.float32, diag_lo, diag_hi)
    mixed = (entries + entries.T) * (0.45 / jnp.sqrt(jnp.float32(order)))
    return mixed + jnp.diag(diagonal)


def draw_anc_inverse(key, part):
    return symmetric_draw(key, NB * B, 1.0, 2.0)


def draw_pivot_inverse(key, part):
    keys = jax.random.split(jax.random.fold_in(key, 29), SUPERNODES)
    return jnp.stack([symmetric_draw(keys[which], B, 1.0, 2.0) for which in range(SUPERNODES)])


def block_scale(rng, shape, cuts, low, high):
    factor_of = 1.0
    for axis_at, parts in cuts:
        draws = jax.random.uniform(jax.random.fold_in(jax.random.fold_in(rng, 6), axis_at), (parts,), jnp.float32, low / len(cuts), high / len(cuts))
        factor_of = factor_of * jnp.repeat(jnp.exp(draws), shape[axis_at] // parts).reshape((-1,) + (1,) * (len(shape) - 1 - axis_at))
    return factor_of


def distinct(rng, rows, count, top, lift):
    sequence = jax.random.permutation(jax.random.fold_in(rng, 1), count)
    favour = sequence
    for power in range(3):
        favour = favour * favour // count
    favour = favour * lift // count
    chance = jax.random.randint(jax.random.fold_in(rng, 2), (rows, count), 0, 4096) + favour
    sure = jax.random.permutation(jax.random.fold_in(rng, 3), rows)[jnp.arange(count) % rows]
    chance = jnp.where(jnp.arange(rows)[:, None] == sure[None, :], 1 << 14, chance)
    score = chance * count + jnp.arange(count)
    return lax.top_k(score.astype(jnp.int32), top)[1].astype(jnp.int32)


def bell_draw(key, extent, scale, reach, shards=(), kind=jnp.bfloat16):
    result = jax.random.normal(key, extent, jnp.float32) * scale
    if len(shards) > 0:
        result = block_scale(key, extent, shards, -0.22, 0.18) * result
    return jnp.clip(result, min=-reach, max=reach).astype(kind)


def setup_inputs(seed: int = 0) -> dict:
    splits = jax.random.split(jax.random.key(seed), 7)
    trailing = bell_draw(splits[0], (NTOT, NTOT), 0.5, 4.0, ((0, 8), (1, 32)), jnp.float32)
    anc_inverse = draw_anc_inverse(jax.random.fold_in(splits[6], 71), 0)
    lower_panels = bell_draw(splits[2], (SUPERNODES, NTOT, B), 1.0, 6.0, ((1, 256),), jnp.float32)
    upper_panels_t = bell_draw(splits[3], (SUPERNODES, NTOT, B), (P_SIZE * B) ** -0.5, 0.078125, ((1, 32), (2, 8)), jnp.float32)
    pivot_inverse = draw_pivot_inverse(jax.random.fold_in(splits[6], 71), 0)
    ancestors = distinct(splits[5], SUPERNODES, NB, P_SIZE, 0)
    return dict(trailing=trailing, anc_inverse=anc_inverse, lower_panels=lower_panels, upper_panels_t=upper_panels_t, pivot_inverse=pivot_inverse, ancestors=ancestors)


def reference(trailing, anc_inverse, lower_panels, upper_panels_t, pivot_inverse, ancestors):
    exact_mode = lax.Precision.HIGHEST
    blocks = jnp.arange(NB * B, dtype=jnp.int32) // B
    masks = jnp.any(blocks[None, :, None] == ancestors[:, None, :], axis=2).astype(jnp.float32)
    schur = trailing
    panels = []
    diagonals = []
    for which in range(SUPERNODES):
        lower_k = lower_panels[which] * masks[which][:, None]
        upper_k = upper_panels_t[which] * masks[which][:, None]
        schur = schur - jnp.dot(lower_k, upper_k.T, precision=exact_mode, preferred_element_type=jnp.float32)
        inverse_k = -jnp.dot(anc_inverse, lower_k, precision=exact_mode, preferred_element_type=jnp.float32) * masks[which][:, None]
        coupling = jnp.dot(upper_k.T, inverse_k, precision=exact_mode, preferred_element_type=jnp.float32)
        diag_k = pivot_inverse[which] - jnp.dot(pivot_inverse[which], coupling, precision=exact_mode, preferred_element_type=jnp.float32)
        panels.append(inverse_k)
        diagonals.append(diag_k)
    return (schur, jnp.stack(panels), jnp.stack(diagonals))
```

```python
import jax
import jax.numpy as jnp
from jax import lax
from jax.sharding import PartitionSpec as P

exact_mode = lax.Precision.HIGH


def copy_for_each(shard, axis):
    copies = jnp.broadcast_to(shard, (lax.axis_size(axis), *shard.shape))
    return lax.all_to_all(copies, axis, split_axis=0, concat_axis=0, tiled=True)


def joined_along(parts, dim):
    dims = list(parts.shape[1:])
    dims[dim] *= parts.shape[0]
    return jnp.moveaxis(parts, 0, dim).reshape(dims)


def collect(shard, axis, dim):
    parts = copy_for_each(shard, axis)
    return joined_along(parts, dim)


def cut_along(shard, dim, devices):
    before, after = (shard.shape[:dim], shard.shape[dim + 1 :])
    return jnp.moveaxis(shard.reshape(*before, devices, -1, *after), dim, 0)


def sum_at_owner(shard, axis, dim):
    devices = lax.axis_size(axis)
    parts = lax.all_to_all(cut_along(shard, dim, devices), axis, 0, 0, tiled=True)
    return jnp.sum(parts, axis=0)


def block_mask(ancestors, first_row, row_count, block_width):
    blocks = (first_row + jnp.arange(row_count, dtype=jnp.int32)) // block_width
    return jnp.any(blocks[None, :, None] == ancestors[:, None, :], axis=2).astype(jnp.float32)


def panel_terms(lower_rows, grid_rows, rows_mask, upper_masked):
    updates = jnp.zeros((grid_rows.shape[0], grid_rows.shape[1]), jnp.float32)
    partials = []
    for which in range(lower_rows.shape[0]):

        def tile_work(lower_k, mask_k, upper_k):
            product = jnp.dot(
                lower_k, upper_k.T, precision=exact_mode, preferred_element_type=jnp.float32
            )
            masked_grid = grid_rows * mask_k[:, None]
            partial_value = lax.dot_general(
                masked_grid,
                lower_k,
                (((0,), (0,)), ((), ())),
                precision=exact_mode,
                preferred_element_type=jnp.float32,
            )
            return (product * mask_k[:, None], partial_value)

        operands = (lower_rows[which], rows_mask[which], upper_masked[which])
        product, partial_value = tile_work(*operands)
        updates = updates + product
        partials.append(partial_value)
    return (updates, jnp.stack(partials))


def body(trailing, anc_inverse, lower_panels, upper_panels_t, pivot_inverse, ancestors):
    rows_here, cols_here = anc_inverse.shape
    panel_width = lower_panels.shape[2]
    row_first = lax.axis_index("prow") * rows_here
    col_first = lax.axis_index("pcol") * cols_here
    row_mask = block_mask(ancestors, row_first, rows_here, panel_width)
    col_mask = block_mask(ancestors, col_first, cols_here, panel_width)
    upper_cols = collect(upper_panels_t, "prow", 2)
    upper_masked = upper_cols * col_mask[:, :, None]
    lower_rows = lax.all_gather(lower_panels, "pcol", axis=1, tiled=True)
    updates, partials = panel_terms(lower_rows, anc_inverse, row_mask, upper_masked)
    schur = trailing - updates
    inverse_local = -sum_at_owner(partials, "prow", 2) * col_mask[:, :, None]
    coupling = jnp.einsum(
        "kcb,kcp->kbp",
        upper_masked,
        inverse_local,
        precision=exact_mode,
        preferred_element_type=jnp.float32,
    )
    coupling_rows = sum_at_owner(coupling, "pcol", 1)
    coupling_full = lax.all_gather(coupling_rows, "pcol", axis=1, tiled=True)
    correction = jnp.einsum(
        "kab,kbp->kap",
        pivot_inverse,
        coupling_full,
        precision=exact_mode,
        preferred_element_type=jnp.float32,
    )
    part_cols = inverse_local.shape[2]
    pivot_slice = lax.dynamic_slice_in_dim(
        pivot_inverse, lax.axis_index("prow") * part_cols, part_cols, 2
    )
    diag_local = pivot_slice - correction
    return (schur, inverse_local, diag_local)


def solution(mesh):
    in_specs = (
        P("prow", "pcol"),
        P("prow", "pcol"),
        P(None, ("prow", "pcol"), None),
        P(None, "pcol", "prow"),
        P(None, "pcol", None),
        P(),
    )
    out_specs = (P("prow", "pcol"), P(None, "pcol", "prow"), P(None, "pcol", "prow"))
    return jax.shard_map(body, mesh=mesh, in_specs=in_specs, out_specs=out_specs, check_vma=False)
```

```python
import functools

import jax
import jax.numpy as jnp
from jax import lax
from jax.experimental import pallas as pl
from jax.experimental.pallas import tpu as pltpu
from jax.sharding import PartitionSpec as P

MESH = pl.DeviceIdType.MESH
F32, BF16 = jnp.float32, jnp.bfloat16
Z, X, C, Y = 8, 2, 2, 4
CHUNKS = 8
DEPTH = 6
SCHUR_LAG = 10
STAGES = (1, 3, 4, 6, 8, 9)
SLOTS = 4 + 3 + DEPTH + STAGES[5] + 1


def split(v):
    hi = v.astype(BF16)
    return hi, (v - hi.astype(F32)).astype(BF16)


def dot(a, b):
    return jnp.dot(a, b, preferred_element_type=F32)


def dot3(ah, al, bh, bl):
    return dot(ah, bh) + (dot(ah, bl) + dot(al, bh))


def kernel(anc_ref, trailing, grid_in, lower, upper, pivot, schur, inv_out, diag_out,
           lb, lhi, llo, gf, gth, gtl, ub, uth, utl, ps, rs, ss, xr, cp, cr, hs, zb, cf, pv,
           s_x, r_x, s_own, r_own, s_a, r_a, s_b, r_b, s_c, r_c, s_u, r_u, s_p, r_p, s_h, r_h,
           s_cc, r_cc, s_z, r_z, s_g, r_g, s_cg, r_cg, loc):
    p, q = lax.axis_index("prow"), lax.axis_index("pcol")
    z, x, c = q // 4, (q // 2) % 2, q % 2
    xh, y = p // 4, p % 4
    zx = z * 2 + x

    def at_q(zz, xx, cc):
        return (p, zz * 4 + xx * 2 + cc)

    def zi(d):
        return (z + d + Z) % Z

    def yi(d):
        return (y + d + Y) % Y

    zp, zm = at_q(zi(1), x, c), at_q(zi(-1), x, c)
    xp, cpart = at_q(z, 1 - x, c), at_q(z, x, 1 - c)
    xhp = ((1 - xh) * 4 + y, q)

    def peer16(d):
        o = (zx + d) % 16
        return at_q(o // 2, o % 2, c)

    def yp(i):
        return (xh * 4 + yi(1 + i), q)

    def rc(src, dst, send, recv, dev):
        return pltpu.make_async_remote_copy(src_ref=src, dst_ref=dst, send_sem=send, recv_sem=recv,
                                            device_id=dev, device_id_type=MESH)

    def row_on(k):
        hits = sum(jnp.where(anc_ref[k, n] == p, 1, 0) for n in range(6))
        return jnp.where(hits > 0, 1.0, 0.0).astype(F32)

    def col_on(k):
        hits = sum(jnp.where(anc_ref[k, n] == q // 4, 1, 0) for n in range(6))
        return jnp.where(hits > 0, 1.0, 0.0).astype(F32)

    barrier = pltpu.get_barrier_semaphore()
    for dev in [peer16(d) for d in range(1, 16)] + [cpart, xhp] + [yp(i) for i in range(3)]:
        pl.semaphore_signal(barrier, inc=1, device_id=dev, device_id_type=MESH)

    def local_copies():
        out = []
        for j in range(CHUNKS):
            k, i = j // 4, j % 4
            for h in range(2):
                col = pl.multiple_of((h * 4 + yi(1 + i)) * 128, 128)
                out.append((lower.at[k, :, pl.ds(col, 128)], lb.at[j, h, z, x, c]))
        for k in range(2):
            out.append((upper.at[k], ub.at[k, p]))
        out.append((grid_in, gf))
        out.append((pivot, pv))
        out.append((trailing, schur))
        return [pltpu.make_async_copy(a, b, loc.at[n]) for n, (a, b) in enumerate(out)]

    locals_ = local_copies()
    for copy in locals_:
        copy.start()
    for copy in locals_[:18]:
        copy.wait()
    pl.semaphore_wait(barrier, 20)

    def own(j, d):
        return lb.at[j, :, zi(d), x, c]

    def pa(j, d):
        return lb.at[j, 0, zi(d), 1 - x, c]

    def own_b(j, d):
        return lb.at[j, 1, zi(d), x, c]

    def pb(j, d):
        return lb.at[j, 1, zi(d), 1 - x, c]

    def send_own(j, d, n, dev):
        return rc(own(j, d), own(j, d), s_own.at[j, n], r_own.at[j, n], dev)

    def wait_own(j, d, n):
        rc(own(j, d), own(j, d), s_own.at[j, n], r_own.at[j, n], zp).wait_recv()

    def send_a(j, d, n, dev):
        return rc(pa(j, d), pa(j, d), s_a.at[j, n], r_a.at[j, n], dev)

    def wait_a(j, d, n):
        rc(pa(j, d), pa(j, d), s_a.at[j, n], r_a.at[j, n], zp).wait_recv()

    def send_b(j, d, n):
        return rc(own_b(j, d), own_b(j, d), s_b.at[j, n], r_b.at[j, n], xp)

    def wait_b(j, d, n):
        rc(pb(j, d), pb(j, d), s_b.at[j, n], r_b.at[j, n], xp).wait_recv()

    def send_c(j, d, n):
        piece = lb.at[j, :, zi(d), :, c]
        return rc(piece, piece, s_c.at[j, n], r_c.at[j, n], cpart)

    def wait_c(j, d, n):
        piece = lb.at[j, :, zi(d), :, 1 - c]
        rc(piece, piece, s_c.at[j, n], r_c.at[j, n], cpart).wait_recv()

    def send_x(j):
        return rc(own(j, 0), own(j, 0), s_x.at[j], r_x.at[j], xp)

    def four(j):
        return 1 - 2 * (j % 2)

    def st0(j):
        send_own(j, 0, 0, zp).start()
        send_own(j, 0, 3, zm).start()
        send_x(j).start()

    def st1(j):
        wait_own(j, -1, 0)
        send_own(j, -1, 1, zp).start()
        wait_own(j, 1, 3)
        send_own(j, 1, 4, zm).start()
        send_b(j, -1, 0).start()
        send_b(j, 1, 3).start()
        part = lb.at[j, :, z, 1 - x, c]
        rc(part, part, s_x.at[j], r_x.at[j], xp).wait_recv()
        send_a(j, 0, 0, zp).start()
        send_a(j, 0, 3, zm).start()
        send_c(j, 0, 7).start()

    def st2(j):
        wait_own(j, -2, 1)
        send_own(j, -2, 2, zp).start()
        wait_own(j, 2, 4)
        send_own(j, 2, 5, zm).start()
        send_b(j, -2, 1).start()
        send_b(j, 2, 4).start()
        wait_a(j, -1, 0)
        send_a(j, -1, 1, zp).start()
        wait_a(j, 1, 3)
        send_a(j, 1, 4, zm).start()
        wait_b(j, -1, 0)
        wait_b(j, 1, 3)
        send_c(j, -1, 0).start()
        send_c(j, 1, 3).start()

    def st3(j):
        wait_own(j, -3, 2)
        wait_own(j, 3, 5)
        sgn = four(j)
        send_own(j, -3 * sgn, 6, at_q(zi(sgn), x, c)).start()
        send_b(j, -3, 2).start()
        send_b(j, 3, 5).start()
        wait_a(j, -2, 1)
        send_a(j, -2, 2, zp).start()
        wait_a(j, 2, 4)
        send_a(j, 2, 5, zm).start()
        wait_b(j, -2, 1)
        wait_b(j, 2, 4)
        send_c(j, -2, 1).start()
        send_c(j, 2, 4).start()

    def st4(j):
        wait_own(j, 4, 6)
        send_b(j, 4, 6).start()
        wait_a(j, -3, 2)
        wait_a(j, 3, 5)
        sgn = -four(j)
        send_a(j, -3 * sgn, 6, at_q(zi(sgn), x, c)).start()
        wait_b(j, -3, 2)
        wait_b(j, 3, 5)
        send_c(j, -3, 2).start()
        send_c(j, 3, 5).start()

    def st5(j):
        wait_a(j, 4, 6)
        wait_b(j, 4, 6)
        send_c(j, 4, 6).start()

    def send_p(j):
        k, i = j // 4, j % 4
        return rc(ps.at[j], rs.at[k, i], s_p.at[k, i], r_p.at[k, i], (xh * 4 + yi(1 + i), q))

    def st6(j):
        for n, d in enumerate((-1, -2, -3, 1, 2, 3, 4, 0)):
            wait_c(j, d, n)
        k, i = j // 4, j % 4

        @pl.loop(0, Z)
        def _(zz):
            rows = pl.ds(pl.multiple_of(zz * 128, 128), 128)
            for h in range(2):
                hi, lo = split(lb[j, h, zz].reshape(128, 128))
                lhi[j, rows, h * 128:(h + 1) * 128] = hi
                llo[j, rows, h * 128:(h + 1) * 128] = lo

        part = dot3(gth[...], gtl[...], lhi[j], llo[j]) * row_on(k)
        ps[j, 0] = part[:, :128]
        ps[j, 1] = part[:, 128:]

        @pl.when(i < 3)
        def _():
            send_p(j).start()

    pxh = (1 - xh) * 4 + y

    def send_u(k, n):
        if n == 0:
            return rc(ub.at[k, p], ub.at[k, p], s_u.at[k, 0], r_u.at[k, 0], xhp)
        i = (n - 1) % 3
        blk = ub.at[k, p] if n < 4 else ub.at[k, pxh]
        return rc(blk, blk, s_u.at[k, n], r_u.at[k, n], yp(i))

    def wait_u(k, n):
        if n == 0:
            src = pxh
        else:
            i = (n - 1) % 3
            src = (xh if n < 4 else 1 - xh) * 4 + yi(-1 - i)
        rc(ub.at[k, src], ub.at[k, src], s_u.at[k, n], r_u.at[k, n], xhp).wait_recv()

    def prepare_grid():
        locals_[18].wait()

        @pl.loop(0, 8)
        def _(zz):
            rows = pl.ds(pl.multiple_of(zz * 128, 128), 128)
            hi, lo = split(gf[rows, :].T)
            gth[:, rows] = hi
            gtl[:, rows] = lo

    def prepare_upper(k):
        for n in range(1, 7):
            wait_u(k, n)

        @pl.loop(0, 8)
        def _(b):
            hi, lo = split(ub[k, b].T)
            uth[k, b] = hi
            utl[k, b] = lo

    def st_schur(j):
        k, i = j // 4, j % 4
        b0, b1 = yi(1 + i), 4 + yi(1 + i)
        uh = jnp.concatenate([uth[k, b0], uth[k, b1]], axis=0)
        ul = jnp.concatenate([utl[k, b0], utl[k, b1]], axis=0)
        scale = row_on(k) * col_on(k)

        @pl.loop(0, 4)
        def _(n):
            rows = pl.ds(pl.multiple_of(n * 256, 256), 256)
            upd = dot3(lhi[j, rows, :], llo[j, rows, :], uh, ul)
            schur[rows, :] = schur[rows, :] - upd * scale

    def send_h(k):
        return rc(ss.at[k], xr.at[k], s_h.at[k], r_h.at[k], xhp)

    def total(k, h):
        return (ps[4 * k + 3, h] + rs[k, 0, h]) + (rs[k, 1, h] + rs[k, 2, h])

    def a0(k):
        for i in range(3):
            rc(ps.at[0], rs.at[k, i], s_p.at[k, i], r_p.at[k, i], xhp).wait_recv()
        ss[k] = total(k, 1 - xh)
        send_h(k).start()

    def send_cc(k):
        return rc(cp.at[k, 1 - c], cr.at[k], s_cc.at[k], r_cc.at[k], cpart)

    def a1(k):
        send_h(k).wait_recv()
        inv = (total(k, xh) + xr[k]) * (-col_on(k))
        inv_out[k] = inv
        hi, lo = split(inv)
        for b in range(8):
            part = dot3(uth[k, b], utl[k, b], hi, lo)
            cp[k, b // 4, (b % 4) * 4:(b % 4) * 4 + 4] = part.reshape(4, 32, 128)
        send_cc(k).start()

    def send_z(k, d):
        return rc(hs.at[k, (zx + d) % 16], zb.at[k, d - 1], s_z.at[k, d - 1], r_z.at[k, d - 1], peer16(d))

    def a2(k):
        send_cc(k).wait_recv()
        hs[k] = cp[k, c] + cr[k]
        for d in (8, 7, 9, 6, 10, 5, 11, 4, 12, 3, 13, 2, 14, 1, 15):
            send_z(k, d).start()

    def send_g(k, d):
        return rc(cf.at[k, c, zx], cf.at[k, c, zx], s_g.at[k, d - 1], r_g.at[k, d - 1], peer16(d))

    def a3(k):
        acc = hs[k, zx]
        for d in range(1, 16):
            send_z(k, d).wait_recv()
        for d in range(15):
            acc = acc + zb[k, d]
        cf[k, c, zx] = acc
        for d in (8, 7, 9, 6, 10, 5, 11, 4, 12, 3, 13, 2, 14, 1, 15):
            send_g(k, d).start()

    def send_cg(k, side):
        return rc(cf.at[k, side], cf.at[k, side], s_cg.at[k], r_cg.at[k], cpart)

    def a4(k):
        for d in range(1, 16):
            src = cf.at[k, c, (zx + 16 - d) % 16]
            rc(src, src, s_g.at[k, d - 1], r_g.at[k, d - 1], cpart).wait_recv()
        send_cg(k, c).start()

    def a5(k):
        send_cg(k, 1 - c).wait_recv()
        ch, cl = split(cf[k].reshape(1024, 128))
        ph, pl_ = split(pv[k])
        mine = pv[k, :, pl.ds(pl.multiple_of(p * 128, 128), 128)]
        diag_out[k] = mine - dot3(ph, pl_, ch, cl)

    stages = (st0, st1, st2, st3, st4, st5, st6)

    def slot(t, carry):
        for o in range(DEPTH, -1, -1):
            if o == 6:
                continue
            j = t - o

            @pl.when((j >= 0) & (j < CHUNKS))
            def _(j=j, o=o):
                stages[o](j)

        @pl.when(t == 0)
        def _():
            for k in range(2):
                for n in range(4):
                    send_u(k, n).start()
            prepare_grid()

        for k in range(2):
            @pl.when(t == 2 + k)
            def _(k=k):
                wait_u(k, 0)
                for n in range(4, 7):
                    send_u(k, n).start()

        j6 = t - DEPTH

        @pl.when((j6 >= 0) & (j6 < CHUNKS))
        def _():
            st6(j6)

        for k in range(2):
            @pl.when(t == 9 + 4 * k)
            def _(k=k):
                prepare_upper(k)

        @pl.when(t == 9)
        def _():
            locals_[19].wait()
            locals_[20].wait()

        for n, fn in enumerate((a0, a1, a2, a3, a4, a5)):
            for k in range(2):
                @pl.when(t == 3 + DEPTH + 4 * k + STAGES[n])
                def _(k=k, fn=fn):
                    fn(k)

        js = t - SCHUR_LAG

        @pl.when((js >= 0) & (js < CHUNKS))
        def _():
            st_schur(js)

        return carry

    lax.fori_loop(0, SLOTS, slot, 0)

    def drain(j, carry):
        for n in range(6):
            send_own(j, 0, n, zp).wait_send()
            send_a(j, 0, n, zp).wait_send()
        send_own(j, 0, 6, zp).wait_send()
        send_a(j, 0, 6, zp).wait_send()
        for n in range(7):
            send_b(j, 0, n).wait_send()
        for n in range(8):
            send_c(j, 0, n).wait_send()
        send_x(j).wait_send()
        return carry

    lax.fori_loop(0, CHUNKS, drain, 0)
    for k in range(2):
        for n in range(7):
            send_u(k, n).wait_send()
        for i in range(3):
            send_p(4 * k + i).wait_send()
        send_h(k).wait_send()
        send_cc(k).wait_send()
        for d in range(1, 16):
            send_z(k, d).wait_send()
            send_g(k, d).wait_send()
        send_cg(k, c).wait_send()


def body(trailing, anc_inverse, lower_panels, upper_panels_t, pivot_inverse, ancestors):
    dma = pltpu.SemaphoreType.DMA
    any_ = pl.BlockSpec(memory_space=pl.ANY)
    vmem = pl.BlockSpec(memory_space=pltpu.VMEM)
    pairs = [(CHUNKS,), (CHUNKS, 7), (CHUNKS, 7), (CHUNKS, 7), (CHUNKS, 8), (2, 7), (2, 3), (2,),
             (2,), (2, 15), (2, 15), (2,)]
    sems = [dma(shape) for shape in pairs for _ in range(2)] + [dma((21,))]
    return pl.pallas_call(
        kernel,
        out_shape=(
            jax.ShapeDtypeStruct((1024, 256), F32),
            jax.ShapeDtypeStruct((2, 256, 128), F32),
            jax.ShapeDtypeStruct((2, 32, 128), F32),
        ),
        in_specs=[pl.BlockSpec(memory_space=pltpu.SMEM), any_, any_, any_, any_, any_],
        out_specs=(vmem, vmem, vmem),
        scratch_shapes=[
            pltpu.VMEM((CHUNKS, 2, Z, X, C, 32, 128), F32),
            pltpu.VMEM((CHUNKS, 1024, 256), BF16),
            pltpu.VMEM((CHUNKS, 1024, 256), BF16),
            pltpu.VMEM((1024, 256), F32),
            pltpu.VMEM((256, 1024), BF16),
            pltpu.VMEM((256, 1024), BF16),
            pltpu.VMEM((2, 8, 256, 128), F32),
            pltpu.VMEM((2, 8, 128, 256), BF16),
            pltpu.VMEM((2, 8, 128, 256), BF16),
            pltpu.VMEM((CHUNKS, 2, 256, 128), F32),
            pltpu.VMEM((2, 3, 2, 256, 128), F32),
            pltpu.VMEM((2, 256, 128), F32),
            pltpu.VMEM((2, 256, 128), F32),
            pltpu.VMEM((2, 2, 16, 32, 128), F32),
            pltpu.VMEM((2, 16, 32, 128), F32),
            pltpu.VMEM((2, 16, 32, 128), F32),
            pltpu.VMEM((2, 15, 32, 128), F32),
            pltpu.VMEM((2, 2, 16, 32, 128), F32),
            pltpu.VMEM((2, 32, 1024), F32),
            *sems,
        ],
        compiler_params=pltpu.CompilerParams(
            collective_id=0, has_side_effects=True, vmem_limit_bytes=56 * 1024 * 1024
        ),
    )(ancestors, trailing, anc_inverse, lower_panels, upper_panels_t, pivot_inverse)


def solution(mesh):
    in_specs = (
        P("prow", "pcol"),
        P("prow", "pcol"),
        P(None, ("prow", "pcol"), None),
        P(None, "pcol", "prow"),
        P(None, "pcol", None),
        P(),
    )
    out_specs = (P("prow", "pcol"), P(None, "pcol", "prow"), P(None, "pcol", "prow"))
    return jax.shard_map(body, mesh=mesh, in_specs=in_specs, out_specs=out_specs, check_vma=False)
```

```python
import functools

import jax
import jax.numpy as jnp
from jax import lax
from jax.experimental import pallas as pl
from jax.experimental.pallas import tpu as pltpu
from jax.sharding import PartitionSpec as P

MESH = pl.DeviceIdType.MESH
F32, BF16 = jnp.float32, jnp.bfloat16
Z, X, C, Y = 8, 2, 2, 4
CHUNKS = 8
PACE = 2
OFF = (0, 3, 6, 9, 12, 15, 16)
DONE = OFF[6]
SCHUR_LAG = DONE + 2
UPPER_AT = (DONE, DONE + 4 * PACE)
STAGES = (2, 5, 6, 9, 12, 13)
UXH_AT = (3, 5)
SLOTS = 7 * PACE + DONE + STAGES[5] + 1


def split(v):
    hi = v.astype(BF16)
    return hi, (v - hi.astype(F32)).astype(BF16)


def dot(a, b):
    return jnp.dot(a, b, preferred_element_type=F32)


def dot3(ah, al, bh, bl):
    return dot(ah, bh) + (dot(ah, bl) + dot(al, bh))


def kernel(anc_ref, trailing, grid_in, lower, upper, pivot, schur, inv_out, diag_out,
           lb, lhi, llo, gf, gth, gtl, ub, uth, utl, ps, rs, ss, xr, cp, cr, hs, zb, cf, pv,
           s_x, s_own, s_a, s_b, s_c, s_u, s_p, s_h, s_cc, s_z, s_g, s_cg,
           r_x, r_own, r_ab, r_c, r_u, r_p, r_h, r_cc, r_z, r_g, r_cg, loc):
    p, q = lax.axis_index("prow"), lax.axis_index("pcol")
    z, x, c = q // 4, (q // 2) % 2, q % 2
    xh, y = p // 4, p % 4
    zx = z * 2 + x

    def at_q(zz, xx, cc):
        return (p, zz * 4 + xx * 2 + cc)

    def zi(d):
        return (z + d + Z) % Z

    def yi(d):
        return (y + d + Y) % Y

    zp, zm = at_q(zi(1), x, c), at_q(zi(-1), x, c)
    xp, cpart = at_q(z, 1 - x, c), at_q(z, x, 1 - c)
    xhp = ((1 - xh) * 4 + y, q)

    def peer16(d):
        o = (zx + d) % 16
        return at_q(o // 2, o % 2, c)

    def yp(i):
        return (xh * 4 + yi(1 + i), q)

    def rc(src, dst, send, recv, dev):
        return pltpu.make_async_remote_copy(src_ref=src, dst_ref=dst, send_sem=send, recv_sem=recv,
                                            device_id=dev, device_id_type=MESH)

    def row_on(k):
        hits = sum(jnp.where(anc_ref[k, n] == p, 1, 0) for n in range(6))
        return jnp.where(hits > 0, 1.0, 0.0).astype(F32)

    def col_on(k):
        hits = sum(jnp.where(anc_ref[k, n] == q // 4, 1, 0) for n in range(6))
        return jnp.where(hits > 0, 1.0, 0.0).astype(F32)

    barrier = pltpu.get_barrier_semaphore()
    for dev in [peer16(d) for d in range(1, 16)] + [cpart, xhp] + [yp(i) for i in range(3)]:
        pl.semaphore_signal(barrier, inc=1, device_id=dev, device_id_type=MESH)

    def local_copies():
        out = []
        for j in range(CHUNKS):
            k, i = j // 4, j % 4
            for h in range(2):
                col = pl.multiple_of((h * 4 + yi(1 + i)) * 128, 128)
                out.append((lower.at[k, :, pl.ds(col, 128)], lb.at[j, h, z, x, c]))
        for k in range(2):
            out.append((upper.at[k], ub.at[k, p]))
        out.append((grid_in, gf))
        out.append((pivot, pv))
        out.append((trailing, schur))
        return [pltpu.make_async_copy(a, b, loc.at[0 if n < 16 else n - 15]) for n, (a, b) in enumerate(out)]

    locals_ = local_copies()
    for copy in locals_:
        copy.start()
    pltpu.make_async_copy(lb.at[0, :, :, 0, 0], lb.at[1, :, :, 0, 0], loc.at[0]).wait()
    for copy in locals_[16:18]:
        copy.wait()
    pl.semaphore_wait(barrier, 20)

    def own(j, d):
        return lb.at[j, :, zi(d), x, c]

    def pa(j, d):
        return lb.at[j, 0, zi(d), 1 - x, c]

    def own_b(j, d):
        return lb.at[j, 1, zi(d), x, c]

    def pb(j, d):
        return lb.at[j, 1, zi(d), 1 - x, c]

    def send_own(j, d, n, dev):
        return rc(own(j, d), own(j, d), s_own.at[j], r_own.at[j, n], dev)

    def send_a(j, d, n, dev):
        return rc(pa(j, d), pa(j, d), s_a.at[j], r_ab.at[j, n], dev)

    def send_b(j, d, n):
        return rc(own_b(j, d), own_b(j, d), s_b.at[j], r_ab.at[j, n], xp)

    def send_c(j, d):
        piece = lb.at[j, :, zi(d), :, c]
        return rc(piece, piece, s_c.at[j], r_c.at[j], cpart)

    def send_x(j):
        return rc(own(j, 0), own(j, 0), s_x.at[j], r_x.at[j], xp)

    def take(sem, view):
        rc(view, view, s_x.at[0], sem, xp).wait_recv()

    def left(sem, view):
        rc(view, view, sem, r_x.at[0], xp).wait_send()

    def four_blocks(j):
        return lb.at[j, :, 0:2, x, c]

    def two_blocks(j):
        return lb.at[j, :, 0, x, c]

    def four(j):
        return 1 - 2 * (j % 2)

    def st0(j):
        send_own(j, 0, 0, zp).start()
        send_own(j, 0, 0, zm).start()
        send_x(j).start()

    def st1(j):
        take(r_own.at[j, 0], four_blocks(j))
        send_own(j, -1, 1, zp).start()
        send_own(j, 1, 1, zm).start()
        take(r_x.at[j], two_blocks(j))
        send_a(j, 0, 0, zp).start()
        send_a(j, 0, 0, zm).start()
        send_b(j, -1, 0).start()
        send_b(j, 1, 0).start()
        send_c(j, 0).start()

    def mid(j, d):
        take(r_own.at[j, d - 1], four_blocks(j))
        if d < 3:
            send_own(j, -d, d, zp).start()
            send_own(j, d, d, zm).start()
        else:
            sgn = four(j)
            send_own(j, -3 * sgn, 3, at_q(zi(sgn), x, c)).start()
        take(r_ab.at[j, d - 2], four_blocks(j))
        send_a(j, -d + 1, d - 1, zp).start()
        send_a(j, d - 1, d - 1, zm).start()
        send_b(j, -d, d - 1).start()
        send_b(j, d, d - 1).start()
        send_c(j, -d + 1).start()
        send_c(j, d - 1).start()

    def st2(j):
        mid(j, 2)

    def st3(j):
        mid(j, 3)

    def st4(j):
        take(r_own.at[j, 3], two_blocks(j))
        send_b(j, 4, 3).start()
        take(r_ab.at[j, 2], four_blocks(j))
        sgn = -four(j)
        send_a(j, -3 * sgn, 3, at_q(zi(sgn), x, c)).start()
        send_c(j, -3).start()
        send_c(j, 3).start()

    def st5(j):
        take(r_ab.at[j, 3], two_blocks(j))
        send_c(j, 4).start()

    def send_p(j):
        k, i = j // 4, j % 4
        return rc(ps.at[j], rs.at[k, i], s_p.at[k], r_p.at[k], (xh * 4 + yi(1 + i), q))

    def st6(j):
        take(r_c.at[j], lb.at[j, :, :, :, 1 - c])
        k, i = j // 4, j % 4

        @pl.loop(0, Z)
        def _(zz):
            rows = pl.ds(pl.multiple_of(zz * 128, 128), 128)
            for h in range(2):
                hi, lo = split(lb[j, h, zz].reshape(128, 128))
                lhi[j, rows, h * 128:(h + 1) * 128] = hi
                llo[j, rows, h * 128:(h + 1) * 128] = lo

        part = dot3(gth[...], gtl[...], lhi[j], llo[j]) * row_on(k)
        ps[j, 0] = part[:, :128]
        ps[j, 1] = part[:, 128:]

        @pl.when(i < 3)
        def _():
            send_p(j).start()

    pxh = (1 - xh) * 4 + y

    def send_u(k, n):
        if n == 0:
            return rc(ub.at[k, p], ub.at[k, p], s_u.at[k], r_u.at[k, 0], xhp)
        i = (n - 1) % 3
        blk = ub.at[k, p] if n < 4 else ub.at[k, pxh]
        return rc(blk, blk, s_u.at[k], r_u.at[k, 1], yp(i))

    def prepare_grid():
        locals_[18].wait()

        @pl.loop(0, 8)
        def _(zz):
            rows = pl.ds(pl.multiple_of(zz * 128, 128), 128)
            hi, lo = split(gf[rows, :].T)
            gth[:, rows] = hi
            gtl[:, rows] = lo

    def prepare_upper(k):
        take(r_u.at[k, 1], ub.at[k, 0:6])

        @pl.loop(0, 8)
        def _(b):
            hi, lo = split(ub[k, b].T)
            uth[k, b] = hi
            utl[k, b] = lo

    def st_schur(j):
        k, i = j // 4, j % 4
        b0, b1 = yi(1 + i), 4 + yi(1 + i)
        uh = jnp.concatenate([uth[k, b0], uth[k, b1]], axis=0)
        ul = jnp.concatenate([utl[k, b0], utl[k, b1]], axis=0)
        scale = row_on(k) * col_on(k)

        @pl.loop(0, 4)
        def _(n):
            rows = pl.ds(pl.multiple_of(n * 256, 256), 256)
            upd = dot3(lhi[j, rows, :], llo[j, rows, :], uh, ul)
            schur[rows, :] = schur[rows, :] - upd * scale

    def send_h(k):
        return rc(ss.at[k], xr.at[k], s_h, r_h.at[k], xhp)

    def total(k, h):
        return (ps[4 * k + 3, h] + rs[k, 0, h]) + (rs[k, 1, h] + rs[k, 2, h])

    def a0(k):
        take(r_p.at[k], rs.at[k])
        ss[k] = total(k, 1 - xh)
        send_h(k).start()

    def send_cc(k):
        return rc(cp.at[k, 1 - c], cr.at[k], s_cc, r_cc.at[k], cpart)

    def a1(k):
        send_h(k).wait_recv()
        inv = (total(k, xh) + xr[k]) * (-col_on(k))
        inv_out[k] = inv
        hi, lo = split(inv)
        for b in range(8):
            part = dot3(uth[k, b], utl[k, b], hi, lo)
            cp[k, b // 4, (b % 4) * 4:(b % 4) * 4 + 4] = part.reshape(4, 32, 128)
        send_cc(k).start()

    def send_z(k, d):
        return rc(hs.at[k, (zx + d) % 16], zb.at[k, d - 1], s_z, r_z.at[k], peer16(d))

    def a2(k):
        send_cc(k).wait_recv()
        hs[k] = cp[k, c] + cr[k]
        for d in (8, 7, 9, 6, 10, 5, 11, 4, 12, 3, 13, 2, 14, 1, 15):
            send_z(k, d).start()

    def send_g(k, d):
        return rc(cf.at[k, c, zx], cf.at[k, c, zx], s_g, r_g.at[k], peer16(d))

    def a3(k):
        acc = hs[k, zx]
        take(r_z.at[k], zb.at[k])
        for d in range(15):
            acc = acc + zb[k, d]
        cf[k, c, zx] = acc
        for d in (8, 7, 9, 6, 10, 5, 11, 4, 12, 3, 13, 2, 14, 1, 15):
            send_g(k, d).start()

    def send_cg(k, side):
        return rc(cf.at[k, side], cf.at[k, side], s_cg, r_cg.at[k], cpart)

    def a4(k):
        take(r_g.at[k], zb.at[k])
        send_cg(k, c).start()

    def a5(k):
        send_cg(k, 1 - c).wait_recv()
        ch, cl = split(cf[k].reshape(1024, 128))
        ph, pl_ = split(pv[k])
        mine = pv[k, :, pl.ds(pl.multiple_of(p * 128, 128), 128)]
        diag_out[k] = mine - dot3(ph, pl_, ch, cl)

    stages = (st0, st1, st2, st3, st4, st5, st6)

    def slot(t, carry):
        for o in range(5, -1, -1):
            tj = t - OFF[o]

            @pl.when((tj >= 0) & (tj % PACE == 0) & (tj < PACE * CHUNKS))
            def _(tj=tj, o=o):
                stages[o](tj // PACE)

        @pl.when(t == 0)
        def _():
            for k in range(2):
                for n in range(4):
                    send_u(k, n).start()
            prepare_grid()

        for k in range(2):
            @pl.when(t == UXH_AT[k])
            def _(k=k):
                take(r_u.at[k, 0], ub.at[k, pxh])
                for n in range(4, 7):
                    send_u(k, n).start()

        t6 = t - DONE

        @pl.when((t6 >= 0) & (t6 % PACE == 0) & (t6 < PACE * CHUNKS))
        def _():
            st6(t6 // PACE)

        for k in range(2):
            @pl.when(t == UPPER_AT[k])
            def _(k=k):
                prepare_upper(k)

        @pl.when(t == DONE)
        def _():
            locals_[19].wait()
            locals_[20].wait()

        for n, fn in enumerate((a0, a1, a2, a3, a4, a5)):
            for k in range(2):
                @pl.when(t == DONE + PACE * (4 * k + 3) + STAGES[n])
                def _(k=k, fn=fn):
                    fn(k)

        ts = t - SCHUR_LAG

        @pl.when((ts >= 0) & (ts % PACE == 0) & (ts < PACE * CHUNKS))
        def _():
            st_schur(ts // PACE)

        return carry

    lax.fori_loop(0, SLOTS, slot, 0)

    def drain(j, carry):
        left(s_own.at[j], lb.at[j, :, 0:7, 0, 0])
        left(s_a.at[j], lb.at[j, 0, 0:7, 0, 0])
        left(s_b.at[j], lb.at[j, 0, 0:7, 0, 0])
        left(s_c.at[j], lb.at[j, :, :, :, 0])
        left(s_x.at[j], two_blocks(j))
        return carry

    lax.fori_loop(0, CHUNKS, drain, 0)
    for k in range(2):
        left(s_u.at[k], ub.at[k, 0:7])
        left(s_p.at[k], rs.at[k])
    left(s_h, ss)
    left(s_cc, cr)
    left(s_z, zb)
    left(s_g, zb)
    left(s_cg, cr)


def body(trailing, anc_inverse, lower_panels, upper_panels_t, pivot_inverse, ancestors):
    dma = pltpu.SemaphoreType.DMA
    any_ = pl.BlockSpec(memory_space=pl.ANY)
    vmem = pl.BlockSpec(memory_space=pltpu.VMEM)
    arrivals = [(CHUNKS,), (CHUNKS, 4), (CHUNKS, 4), (CHUNKS,), (2, 2)] + [(2,)] * 6
    sems = [dma((CHUNKS,))] * 5 + [dma((2,))] * 2 + [dma] * 5 + [dma(shape) for shape in arrivals] + [dma((6,))]
    return pl.pallas_call(
        kernel,
        out_shape=(
            jax.ShapeDtypeStruct((1024, 256), F32),
            jax.ShapeDtypeStruct((2, 256, 128), F32),
            jax.ShapeDtypeStruct((2, 32, 128), F32),
        ),
        in_specs=[pl.BlockSpec(memory_space=pltpu.SMEM), any_, any_, any_, any_, any_],
        out_specs=(vmem, vmem, vmem),
        scratch_shapes=[
            pltpu.VMEM((CHUNKS, 2, Z, X, C, 32, 128), F32),
            pltpu.VMEM((CHUNKS, 1024, 256), BF16),
            pltpu.VMEM((CHUNKS, 1024, 256), BF16),
            pltpu.VMEM((1024, 256), F32),
            pltpu.VMEM((256, 1024), BF16),
            pltpu.VMEM((256, 1024), BF16),
            pltpu.VMEM((2, 8, 256, 128), F32),
            pltpu.VMEM((2, 8, 128, 256), BF16),
            pltpu.VMEM((2, 8, 128, 256), BF16),
            pltpu.VMEM((CHUNKS, 2, 256, 128), F32),
            pltpu.VMEM((2, 3, 2, 256, 128), F32),
            pltpu.VMEM((2, 256, 128), F32),
            pltpu.VMEM((2, 256, 128), F32),
            pltpu.VMEM((2, 2, 16, 32, 128), F32),
            pltpu.VMEM((2, 16, 32, 128), F32),
            pltpu.VMEM((2, 16, 32, 128), F32),
            pltpu.VMEM((2, 15, 32, 128), F32),
            pltpu.VMEM((2, 2, 16, 32, 128), F32),
            pltpu.VMEM((2, 32, 1024), F32),
            *sems,
        ],
        compiler_params=pltpu.CompilerParams(
            collective_id=0, has_side_effects=True, vmem_limit_bytes=56 * 1024 * 1024
        ),
    )(ancestors, trailing, anc_inverse, lower_panels, upper_panels_t, pivot_inverse)


def solution(mesh):
    in_specs = (
        P("prow", "pcol"),
        P("prow", "pcol"),
        P(None, ("prow", "pcol"), None),
        P(None, "pcol", "prow"),
        P(None, "pcol", None),
        P(),
    )
    out_specs = (P("prow", "pcol"), P(None, "pcol", "prow"), P(None, "pcol", "prow"))
    return jax.shard_map(body, mesh=mesh, in_specs=in_specs, out_specs=out_specs, check_vma=False)
```

```python
import functools

import jax
import jax.numpy as jnp
from jax import lax
from jax.experimental import pallas as pl
from jax.experimental.pallas import tpu as pltpu
from jax.sharding import PartitionSpec as P

MESH = pl.DeviceIdType.MESH
F32, BF16 = jnp.float32, jnp.bfloat16
Z, X, C, Y = 8, 2, 2, 4
CHUNKS = 8
PACE = 3
OFF = (0, 4, 8, 12, 16, 20, 21)
DONE = OFF[6]
SCHUR_LAG = DONE + 2
UPPER_AT = (DONE, DONE + 4 * PACE)
STAGES = (3, 8, 10, 15, 20, 23)
UXH_AT = (4, 6)
SLOTS = 7 * PACE + DONE + STAGES[5] + 1


def split(v):
    hi = v.astype(BF16)
    return hi, (v - hi.astype(F32)).astype(BF16)


def dot(a, b):
    return jnp.dot(a, b, preferred_element_type=F32)


def dot3(ah, al, bh, bl):
    return dot(ah, bh) + (dot(ah, bl) + dot(al, bh))


def kernel(anc_ref, trailing, grid_in, lower, upper, pivot, schur, inv_out, diag_out,
           lb, lhi, llo, gf, gth, gtl, ub, uth, utl, ps, rs, ss, xr, cp, cr, hs, zb, cf, pv,
           s_x, s_own, s_a, s_b, s_c, s_u, s_p, s_h, s_cc, s_z, s_g, s_cg,
           r_x, r_own, r_ab, r_c, r_u, r_p, r_h, r_cc, r_z, r_g, r_cg, loc):
    p, q = lax.axis_index("prow"), lax.axis_index("pcol")
    z, x, c = q // 4, (q // 2) % 2, q % 2
    xh, y = p // 4, p % 4
    zx = z * 2 + x

    def at_q(zz, xx, cc):
        return (p, zz * 4 + xx * 2 + cc)

    def zi(d):
        return (z + d + Z) % Z

    def yi(d):
        return (y + d + Y) % Y

    zp, zm = at_q(zi(1), x, c), at_q(zi(-1), x, c)
    xp, cpart = at_q(z, 1 - x, c), at_q(z, x, 1 - c)
    xhp = ((1 - xh) * 4 + y, q)

    def peer16(d):
        o = (zx + d) % 16
        return at_q(o // 2, o % 2, c)

    def yp(i):
        return (xh * 4 + yi(1 + i), q)

    def ahead(i):
        return i + 1 + jnp.where(i == 0, 1, 0) - jnp.where(i == 1, 1, 0)

    def rc(src, dst, send, recv, dev):
        return pltpu.make_async_remote_copy(src_ref=src, dst_ref=dst, send_sem=send, recv_sem=recv,
                                            device_id=dev, device_id_type=MESH)

    def row_on(k):
        hits = sum(jnp.where(anc_ref[k, n] == p, 1, 0) for n in range(6))
        return jnp.where(hits > 0, 1.0, 0.0).astype(F32)

    def col_on(k):
        hits = sum(jnp.where(anc_ref[k, n] == q // 4, 1, 0) for n in range(6))
        return jnp.where(hits > 0, 1.0, 0.0).astype(F32)

    barrier = pltpu.get_barrier_semaphore()
    for dev in [peer16(d) for d in range(1, 16)] + [cpart, xhp] + [yp(i) for i in range(3)]:
        pl.semaphore_signal(barrier, inc=1, device_id=dev, device_id_type=MESH)

    def local_copies():
        out = []
        for j in range(CHUNKS):
            k, i = j // 4, j % 4
            for h in range(2):
                col = pl.multiple_of((h * 4 + yi((2, 1, 3, 4)[i])) * 128, 128)
                out.append((lower.at[k, :, pl.ds(col, 128)], lb.at[j, h, z, x, c]))
        for k in range(2):
            out.append((upper.at[k], ub.at[k, p]))
        out.append((grid_in, gf))
        out.append((pivot, pv))
        out.append((trailing, schur))
        return [pltpu.make_async_copy(a, b, loc.at[0 if n < 16 else n - 15]) for n, (a, b) in enumerate(out)]

    locals_ = local_copies()
    for copy in locals_:
        copy.start()
    pltpu.make_async_copy(lb.at[0, :, :, 0, 0], lb.at[1, :, :, 0, 0], loc.at[0]).wait()
    for copy in locals_[16:18]:
        copy.wait()
    pl.semaphore_wait(barrier, 20)

    def own(j, d):
        return lb.at[j, :, zi(d), x, c]

    def pa(j, d):
        return lb.at[j, 0, zi(d), 1 - x, c]

    def own_b(j, d):
        return lb.at[j, 1, zi(d), x, c]

    def pb(j, d):
        return lb.at[j, 1, zi(d), 1 - x, c]

    def send_own(j, d, n, dev):
        return rc(own(j, d), own(j, d), s_own.at[j], r_own.at[j, n], dev)

    def send_a(j, d, n, dev):
        return rc(pa(j, d), pa(j, d), s_a.at[j], r_ab.at[j, n], dev)

    def send_b(j, d, n):
        return rc(own_b(j, d), own_b(j, d), s_b.at[j], r_ab.at[j, n], xp)

    def send_c(j, d):
        piece = lb.at[j, :, zi(d), :, c]
        return rc(piece, piece, s_c.at[j], r_c.at[j], cpart)

    def send_x(j):
        return rc(own(j, 0), own(j, 0), s_x.at[j], r_x.at[j], xp)

    def take(sem, view):
        rc(view, view, s_x.at[0], sem, xp).wait_recv()

    def left(sem, view):
        rc(view, view, sem, r_x.at[0], xp).wait_send()

    def four_blocks(j):
        return lb.at[j, :, 0:2, x, c]

    def two_blocks(j):
        return lb.at[j, :, 0, x, c]

    def four(j):
        return 1 - 2 * (j % 2)

    def st0(j):
        send_own(j, 0, 0, zp).start()
        send_own(j, 0, 0, zm).start()
        send_x(j).start()

    def st1(j):
        take(r_own.at[j, 0], four_blocks(j))
        send_own(j, -1, 1, zp).start()
        send_own(j, 1, 1, zm).start()
        take(r_x.at[j], two_blocks(j))
        send_a(j, 0, 0, zp).start()
        send_a(j, 0, 0, zm).start()
        send_b(j, -1, 0).start()
        send_b(j, 1, 0).start()
        send_c(j, 0).start()

    def mid(j, d):
        take(r_own.at[j, d - 1], four_blocks(j))
        if d < 3:
            send_own(j, -d, d, zp).start()
            send_own(j, d, d, zm).start()
        else:
            sgn = four(j)
            send_own(j, -3 * sgn, 3, at_q(zi(sgn), x, c)).start()
        take(r_ab.at[j, d - 2], four_blocks(j))
        send_a(j, -d + 1, d - 1, zp).start()
        send_a(j, d - 1, d - 1, zm).start()
        send_b(j, -d, d - 1).start()
        send_b(j, d, d - 1).start()
        send_c(j, -d + 1).start()
        send_c(j, d - 1).start()

    def st2(j):
        mid(j, 2)

    def st3(j):
        mid(j, 3)

    def st4(j):
        take(r_own.at[j, 3], two_blocks(j))
        send_b(j, 4, 3).start()
        take(r_ab.at[j, 2], four_blocks(j))
        sgn = -four(j)
        send_a(j, -3 * sgn, 3, at_q(zi(sgn), x, c)).start()
        send_c(j, -3).start()
        send_c(j, 3).start()

    def st5(j):
        take(r_ab.at[j, 3], two_blocks(j))
        send_c(j, 4).start()

    def send_p(j):
        k, i = j // 4, j % 4
        return rc(ps.at[j], rs.at[k, i], s_p.at[k], r_p.at[k], (xh * 4 + yi(ahead(i)), q))

    def st6(j):
        take(r_c.at[j], lb.at[j, :, :, :, 1 - c])
        k, i = j // 4, j % 4

        @pl.loop(0, Z)
        def _(zz):
            rows = pl.ds(pl.multiple_of(zz * 128, 128), 128)
            for h in range(2):
                hi, lo = split(lb[j, h, zz].reshape(128, 128))
                lhi[j, rows, h * 128:(h + 1) * 128] = hi
                llo[j, rows, h * 128:(h + 1) * 128] = lo

        part = dot3(gth[...], gtl[...], lhi[j], llo[j]) * row_on(k)
        ps[j, 0] = part[:, :128]
        ps[j, 1] = part[:, 128:]

        @pl.when(i < 3)
        def _():
            send_p(j).start()

    pxh = (1 - xh) * 4 + y

    def send_u(k, n):
        if n == 0:
            return rc(ub.at[k, p], ub.at[k, p], s_u.at[k], r_u.at[k, 0], xhp)
        i = (n - 1) % 3
        blk = ub.at[k, p] if n < 4 else ub.at[k, pxh]
        return rc(blk, blk, s_u.at[k], r_u.at[k, 1], yp(i))

    def prepare_grid():
        locals_[18].wait()

        @pl.loop(0, 8)
        def _(zz):
            rows = pl.ds(pl.multiple_of(zz * 128, 128), 128)
            hi, lo = split(gf[rows, :].T)
            gth[:, rows] = hi
            gtl[:, rows] = lo

    def prepare_upper(k):
        take(r_u.at[k, 1], ub.at[k, 0:6])

        @pl.loop(0, 8)
        def _(b):
            hi, lo = split(ub[k, b].T)
            uth[k, b] = hi
            utl[k, b] = lo

    def st_schur(j):
        k, i = j // 4, j % 4
        b0, b1 = yi(ahead(i)), 4 + yi(ahead(i))
        uh = jnp.concatenate([uth[k, b0], uth[k, b1]], axis=0)
        ul = jnp.concatenate([utl[k, b0], utl[k, b1]], axis=0)
        scale = row_on(k) * col_on(k)

        @pl.loop(0, 4)
        def _(n):
            rows = pl.ds(pl.multiple_of(n * 256, 256), 256)
            upd = dot3(lhi[j, rows, :], llo[j, rows, :], uh, ul)
            schur[rows, :] = schur[rows, :] - upd * scale

    def send_h(k):
        return rc(ss.at[k], xr.at[k], s_h, r_h.at[k], xhp)

    def total(k, h):
        return (ps[4 * k + 3, h] + rs[k, 0, h]) + (rs[k, 1, h] + rs[k, 2, h])

    def a0(k):
        take(r_p.at[k], rs.at[k])
        ss[k] = total(k, 1 - xh)
        send_h(k).start()

    def send_cc(k):
        return rc(cp.at[k, 1 - c], cr.at[k], s_cc, r_cc.at[k], cpart)

    def a1(k):
        send_h(k).wait_recv()
        inv = (total(k, xh) + xr[k]) * (-col_on(k))
        inv_out[k] = inv
        hi, lo = split(inv)
        for b in range(8):
            part = dot3(uth[k, b], utl[k, b], hi, lo)
            cp[k, b // 4, (b % 4) * 4:(b % 4) * 4 + 4] = part.reshape(4, 32, 128)
        send_cc(k).start()

    def send_z(k, d):
        return rc(hs.at[k, (zx + d) % 16], zb.at[k, d - 1], s_z, r_z.at[k], peer16(d))

    def a2(k):
        send_cc(k).wait_recv()
        hs[k] = cp[k, c] + cr[k]
        for d in (8, 7, 9, 6, 10, 5, 11, 4, 12, 3, 13, 2, 14, 1, 15):
            send_z(k, d).start()

    def send_g(k, d):
        return rc(cf.at[k, c, zx], cf.at[k, c, zx], s_g, r_g.at[k], peer16(d))

    def a3(k):
        acc = hs[k, zx]
        take(r_z.at[k], zb.at[k])
        for d in range(15):
            acc = acc + zb[k, d]
        cf[k, c, zx] = acc
        for d in (8, 7, 9, 6, 10, 5, 11, 4, 12, 3, 13, 2, 14, 1, 15):
            send_g(k, d).start()

    def send_cg(k, side):
        return rc(cf.at[k, side], cf.at[k, side], s_cg, r_cg.at[k], cpart)

    def a4(k):
        take(r_g.at[k], zb.at[k])
        send_cg(k, c).start()

    def a5(k):
        send_cg(k, 1 - c).wait_recv()
        ch, cl = split(cf[k].reshape(1024, 128))
        ph, pl_ = split(pv[k])
        mine = pv[k, :, pl.ds(pl.multiple_of(p * 128, 128), 128)]
        diag_out[k] = mine - dot3(ph, pl_, ch, cl)

    stages = (st0, st1, st2, st3, st4, st5, st6)

    def slot(t, carry):
        for o in range(5, -1, -1):
            tj = t - OFF[o]

            @pl.when((tj >= 0) & (tj % PACE == 0) & (tj < PACE * CHUNKS))
            def _(tj=tj, o=o):
                stages[o](tj // PACE)

        @pl.when(t == 0)
        def _():
            for k in range(2):
                for n in range(4):
                    send_u(k, n).start()
            prepare_grid()

        for k in range(2):
            @pl.when(t == UXH_AT[k])
            def _(k=k):
                take(r_u.at[k, 0], ub.at[k, pxh])
                for n in range(4, 7):
                    send_u(k, n).start()

        t6 = t - DONE

        @pl.when((t6 >= 0) & (t6 % PACE == 0) & (t6 < PACE * CHUNKS))
        def _():
            st6(t6 // PACE)

        for k in range(2):
            @pl.when(t == UPPER_AT[k])
            def _(k=k):
                prepare_upper(k)

        @pl.when(t == DONE)
        def _():
            locals_[19].wait()
            locals_[20].wait()

        for n, fn in enumerate((a0, a1, a2, a3, a4, a5)):
            for k in range(2):
                @pl.when(t == DONE + PACE * (4 * k + 3) + STAGES[n])
                def _(k=k, fn=fn):
                    fn(k)

        ts = t - SCHUR_LAG

        @pl.when((ts >= 0) & (ts % PACE == 0) & (ts < PACE * CHUNKS))
        def _():
            st_schur(ts // PACE)

        return carry

    lax.fori_loop(0, SLOTS, slot, 0)

    def drain(j, carry):
        left(s_own.at[j], lb.at[j, :, 0:7, 0, 0])
        left(s_a.at[j], lb.at[j, 0, 0:7, 0, 0])
        left(s_b.at[j], lb.at[j, 0, 0:7, 0, 0])
        left(s_c.at[j], lb.at[j, :, :, :, 0])
        left(s_x.at[j], two_blocks(j))
        return carry

    lax.fori_loop(0, CHUNKS, drain, 0)
    for k in range(2):
        left(s_u.at[k], ub.at[k, 0:7])
        left(s_p.at[k], rs.at[k])
    left(s_h, ss)
    left(s_cc, cr)
    left(s_z, zb)
    left(s_g, zb)
    left(s_cg, cr)


def body(trailing, anc_inverse, lower_panels, upper_panels_t, pivot_inverse, ancestors):
    dma = pltpu.SemaphoreType.DMA
    any_ = pl.BlockSpec(memory_space=pl.ANY)
    vmem = pl.BlockSpec(memory_space=pltpu.VMEM)
    arrivals = [(CHUNKS,), (CHUNKS, 4), (CHUNKS, 4), (CHUNKS,), (2, 2)] + [(2,)] * 6
    sems = [dma((CHUNKS,))] * 5 + [dma((2,))] * 2 + [dma] * 5 + [dma(shape) for shape in arrivals] + [dma((6,))]
    return pl.pallas_call(
        kernel,
        out_shape=(
            jax.ShapeDtypeStruct((1024, 256), F32),
            jax.ShapeDtypeStruct((2, 256, 128), F32),
            jax.ShapeDtypeStruct((2, 32, 128), F32),
        ),
        in_specs=[pl.BlockSpec(memory_space=pltpu.SMEM), any_, any_, any_, any_, any_],
        out_specs=(vmem, vmem, vmem),
        scratch_shapes=[
            pltpu.VMEM((CHUNKS, 2, Z, X, C, 32, 128), F32),
            pltpu.VMEM((CHUNKS, 1024, 256), BF16),
            pltpu.VMEM((CHUNKS, 1024, 256), BF16),
            pltpu.VMEM((1024, 256), F32),
            pltpu.VMEM((256, 1024), BF16),
            pltpu.VMEM((256, 1024), BF16),
            pltpu.VMEM((2, 8, 256, 128), F32),
            pltpu.VMEM((2, 8, 128, 256), BF16),
            pltpu.VMEM((2, 8, 128, 256), BF16),
            pltpu.VMEM((CHUNKS, 2, 256, 128), F32),
            pltpu.VMEM((2, 3, 2, 256, 128), F32),
            pltpu.VMEM((2, 256, 128), F32),
            pltpu.VMEM((2, 256, 128), F32),
            pltpu.VMEM((2, 2, 16, 32, 128), F32),
            pltpu.VMEM((2, 16, 32, 128), F32),
            pltpu.VMEM((2, 16, 32, 128), F32),
            pltpu.VMEM((2, 15, 32, 128), F32),
            pltpu.VMEM((2, 2, 16, 32, 128), F32),
            pltpu.VMEM((2, 32, 1024), F32),
            *sems,
        ],
        compiler_params=pltpu.CompilerParams(
            collective_id=0, has_side_effects=True, vmem_limit_bytes=56 * 1024 * 1024
        ),
    )(ancestors, trailing, anc_inverse, lower_panels, upper_panels_t, pivot_inverse)


def solution(mesh):
    in_specs = (
        P("prow", "pcol"),
        P("prow", "pcol"),
        P(None, ("prow", "pcol"), None),
        P(None, "pcol", "prow"),
        P(None, "pcol", None),
        P(),
    )
    out_specs = (P("prow", "pcol"), P(None, "pcol", "prow"), P(None, "pcol", "prow"))
    return jax.shard_map(body, mesh=mesh, in_specs=in_specs, out_specs=out_specs, check_vma=False)
```

```python
import functools

import jax
import jax.numpy as jnp
from jax import lax
from jax.experimental import pallas as pl
from jax.experimental.pallas import tpu as pltpu
from jax.sharding import PartitionSpec as P

MESH = pl.DeviceIdType.MESH
F32, BF16 = jnp.float32, jnp.bfloat16
Z, X, C, Y = 8, 2, 2, 4
CHUNKS = 8
PACE = 3
OFF = (0, 4, 8, 12, 16, 20, 21)
DONE = OFF[6]
SCHUR_LAG = DONE + 2
UPPER_AT = (DONE, DONE + 4 * PACE)
STAGES = (3, 8, 10, 15, 20, 23)
UXH_AT = (4, 6)
SLOTS = 7 * PACE + DONE + STAGES[5] + 1


def split(v):
    hi = v.astype(BF16)
    return hi, (v - hi.astype(F32)).astype(BF16)


def dot(a, b):
    return jnp.dot(a, b, preferred_element_type=F32)


def dot3(ah, al, bh, bl):
    return dot(ah, bh) + (dot(ah, bl) + dot(al, bh))


def kernel(anc_ref, trailing, grid_in, lower, upper, pivot, schur, inv_out, diag_out,
           lb, lhi, llo, gf, gth, gtl, ub, uth, utl, ps, rs, ss, xr, cp, cr, hs, zb, cf, pv,
           s_x, s_own, s_a, s_b, s_c, s_u, s_p, s_h, s_cc, s_z, s_g, s_cg,
           r_x, r_own, r_ab, r_c, r_u, r_p, r_h, r_cc, r_z, r_g, r_cg, loc):
    p, q = lax.axis_index("prow"), lax.axis_index("pcol")
    z, x, c = q // 4, (q // 2) % 2, q % 2
    xh, y = p // 4, p % 4
    zx = z * 2 + x

    def at_q(zz, xx, cc):
        return (p, zz * 4 + xx * 2 + cc)

    def zi(d):
        return (z + d + Z) % Z

    def yi(d):
        return (y + d + Y) % Y

    zp, zm = at_q(zi(1), x, c), at_q(zi(-1), x, c)
    xp, cpart = at_q(z, 1 - x, c), at_q(z, x, 1 - c)
    xhp = ((1 - xh) * 4 + y, q)

    def peer16(d):
        o = (zx + d) % 16
        return at_q(o // 2, o % 2, c)

    def yp(i):
        return (xh * 4 + yi(1 + i), q)

    def ahead(i):
        return i + 1 + jnp.where(i == 0, 1, 0) - jnp.where(i == 1, 1, 0)

    def rc(src, dst, send, recv, dev):
        return pltpu.make_async_remote_copy(src_ref=src, dst_ref=dst, send_sem=send, recv_sem=recv,
                                            device_id=dev, device_id_type=MESH)

    def row_on(k):
        hits = sum(jnp.where(anc_ref[k, n] == p, 1, 0) for n in range(6))
        return jnp.where(hits > 0, 1.0, 0.0).astype(F32)

    def col_on(k):
        hits = sum(jnp.where(anc_ref[k, n] == q // 4, 1, 0) for n in range(6))
        return jnp.where(hits > 0, 1.0, 0.0).astype(F32)

    barrier = pltpu.get_barrier_semaphore()
    for dev in [zp, zm, xp, cpart, xhp] + [yp(i) for i in range(3)]:
        pl.semaphore_signal(barrier, inc=1, device_id=dev, device_id_type=MESH)

    def local_copies():
        out = []
        for j in range(CHUNKS):
            k, i = j // 4, j % 4
            for h in range(2):
                col = pl.multiple_of((h * 4 + yi((2, 1, 3, 4)[i])) * 128, 128)
                out.append((lower.at[k, :, pl.ds(col, 128)], lb.at[j, h, z, x, c]))
        for k in range(2):
            out.append((upper.at[k], ub.at[k, p]))
        out.append((grid_in, gf))
        out.append((pivot, pv))
        out.append((trailing, schur))
        return [pltpu.make_async_copy(a, b, loc.at[0 if n < 16 else n - 15]) for n, (a, b) in enumerate(out)]

    locals_ = local_copies()
    for copy in locals_:
        copy.start()
    pltpu.make_async_copy(lb.at[0, :, :, 0, 0], lb.at[1, :, :, 0, 0], loc.at[0]).wait()
    for copy in locals_[16:18]:
        copy.wait()
    pl.semaphore_wait(barrier, 8)

    def own(j, d):
        return lb.at[j, :, zi(d), x, c]

    def pa(j, d):
        return lb.at[j, 0, zi(d), 1 - x, c]

    def own_b(j, d):
        return lb.at[j, 1, zi(d), x, c]

    def pb(j, d):
        return lb.at[j, 1, zi(d), 1 - x, c]

    def send_own(j, d, n, dev):
        return rc(own(j, d), own(j, d), s_own.at[j], r_own.at[j, n], dev)

    def send_a(j, d, n, dev):
        return rc(pa(j, d), pa(j, d), s_a.at[j], r_ab.at[j, n], dev)

    def send_b(j, d, n):
        return rc(own_b(j, d), own_b(j, d), s_b.at[j], r_ab.at[j, n], xp)

    def send_c(j, d):
        piece = lb.at[j, :, zi(d), :, c]
        return rc(piece, piece, s_c.at[j], r_c.at[j], cpart)

    def send_x(j):
        return rc(own(j, 0), own(j, 0), s_x.at[j], r_x.at[j], xp)

    def take(sem, view):
        rc(view, view, s_x.at[0], sem, xp).wait_recv()

    def left(sem, view):
        rc(view, view, sem, r_x.at[0], xp).wait_send()

    def four_blocks(j):
        return lb.at[j, :, 0:2, x, c]

    def two_blocks(j):
        return lb.at[j, :, 0, x, c]

    def four(j):
        return 1 - 2 * (j % 2)

    def st0(j):
        send_own(j, 0, 0, zp).start()
        send_own(j, 0, 0, zm).start()
        send_x(j).start()

    def st1(j):
        take(r_own.at[j, 0], four_blocks(j))
        send_own(j, -1, 1, zp).start()
        send_own(j, 1, 1, zm).start()
        take(r_x.at[j], two_blocks(j))
        send_a(j, 0, 0, zp).start()
        send_a(j, 0, 0, zm).start()
        send_b(j, -1, 0).start()
        send_b(j, 1, 0).start()
        send_c(j, 0).start()

    def mid(j, d):
        take(r_own.at[j, d - 1], four_blocks(j))
        if d < 3:
            send_own(j, -d, d, zp).start()
            send_own(j, d, d, zm).start()
        else:
            sgn = four(j)
            send_own(j, -3 * sgn, 3, at_q(zi(sgn), x, c)).start()
        take(r_ab.at[j, d - 2], four_blocks(j))
        send_a(j, -d + 1, d - 1, zp).start()
        send_a(j, d - 1, d - 1, zm).start()
        send_b(j, -d, d - 1).start()
        send_b(j, d, d - 1).start()
        send_c(j, -d + 1).start()
        send_c(j, d - 1).start()

    def st2(j):
        mid(j, 2)

    def st3(j):
        mid(j, 3)

    def st4(j):
        take(r_own.at[j, 3], two_blocks(j))
        send_b(j, 4, 3).start()
        take(r_ab.at[j, 2], four_blocks(j))
        sgn = -four(j)
        send_a(j, -3 * sgn, 3, at_q(zi(sgn), x, c)).start()
        send_c(j, -3).start()
        send_c(j, 3).start()

    def st5(j):
        take(r_ab.at[j, 3], two_blocks(j))
        send_c(j, 4).start()

    def send_p(j):
        k, i = j // 4, j % 4
        return rc(ps.at[j], rs.at[k, i], s_p.at[k], r_p.at[k], (xh * 4 + yi(ahead(i)), q))

    def st6(j):
        take(r_c.at[j], lb.at[j, :, :, :, 1 - c])
        k, i = j // 4, j % 4

        @pl.loop(0, Z)
        def _(zz):
            rows = pl.ds(pl.multiple_of(zz * 128, 128), 128)
            for h in range(2):
                hi, lo = split(lb[j, h, zz].reshape(128, 128))
                lhi[j, rows, h * 128:(h + 1) * 128] = hi
                llo[j, rows, h * 128:(h + 1) * 128] = lo

        part = dot3(gth[...], gtl[...], lhi[j], llo[j]) * row_on(k)
        ps[j, 0] = part[:, :128]
        ps[j, 1] = part[:, 128:]

        @pl.when(i < 3)
        def _():
            send_p(j).start()

    pxh = (1 - xh) * 4 + y

    def send_u(k, n):
        if n == 0:
            return rc(ub.at[k, p], ub.at[k, p], s_u.at[k], r_u.at[k, 0], xhp)
        i = (n - 1) % 3
        blk = ub.at[k, p] if n < 4 else ub.at[k, pxh]
        return rc(blk, blk, s_u.at[k], r_u.at[k, 1], yp(i))

    def prepare_grid():
        locals_[18].wait()

        @pl.loop(0, 8)
        def _(zz):
            rows = pl.ds(pl.multiple_of(zz * 128, 128), 128)
            hi, lo = split(gf[rows, :].T)
            gth[:, rows] = hi
            gtl[:, rows] = lo

    def prepare_upper(k):
        take(r_u.at[k, 1], ub.at[k, 0:6])

        @pl.loop(0, 8)
        def _(b):
            hi, lo = split(ub[k, b].T)
            uth[k, b] = hi
            utl[k, b] = lo

    def st_schur(j):
        k, i = j // 4, j % 4
        b0, b1 = yi(ahead(i)), 4 + yi(ahead(i))
        uh = jnp.concatenate([uth[k, b0], uth[k, b1]], axis=0)
        ul = jnp.concatenate([utl[k, b0], utl[k, b1]], axis=0)
        scale = row_on(k) * col_on(k)

        @pl.loop(0, 4)
        def _(n):
            rows = pl.ds(pl.multiple_of(n * 256, 256), 256)
            upd = dot3(lhi[j, rows, :], llo[j, rows, :], uh, ul)
            schur[rows, :] = schur[rows, :] - upd * scale

    def send_h(k):
        return rc(ss.at[k], xr.at[k], s_h, r_h.at[k], xhp)

    def total(k, h):
        return (ps[4 * k + 3, h] + rs[k, 0, h]) + (rs[k, 1, h] + rs[k, 2, h])

    def a0(k):
        take(r_p.at[k], rs.at[k])
        ss[k] = total(k, 1 - xh)
        send_h(k).start()

    def send_cc(k):
        return rc(cp.at[k, 1 - c], cr.at[k], s_cc, r_cc.at[k], cpart)

    def a1(k):
        send_h(k).wait_recv()
        inv = (total(k, xh) + xr[k]) * (-col_on(k))
        inv_out[k] = inv
        hi, lo = split(inv)
        for b in range(8):
            part = dot3(uth[k, b], utl[k, b], hi, lo)
            cp[k, b // 4, (b % 4) * 4:(b % 4) * 4 + 4] = part.reshape(4, 32, 128)
        send_cc(k).start()

    def send_z(k, d):
        return rc(hs.at[k, (zx + d) % 16], zb.at[k, d - 1], s_z, r_z.at[k], peer16(d))

    def a2(k):
        send_cc(k).wait_recv()
        hs[k] = cp[k, c] + cr[k]
        for d in (8, 7, 9, 6, 10, 5, 11, 4, 12, 3, 13, 2, 14, 1, 15):
            send_z(k, d).start()

    def send_g(k, d):
        return rc(cf.at[k, c, zx], cf.at[k, c, zx], s_g, r_g.at[k], peer16(d))

    def a3(k):
        acc = hs[k, zx]
        take(r_z.at[k], zb.at[k])
        for d in range(15):
            acc = acc + zb[k, d]
        cf[k, c, zx] = acc
        for d in (8, 7, 9, 6, 10, 5, 11, 4, 12, 3, 13, 2, 14, 1, 15):
            send_g(k, d).start()

    def send_cg(k, side):
        return rc(cf.at[k, side], cf.at[k, side], s_cg, r_cg.at[k], cpart)

    def a4(k):
        take(r_g.at[k], zb.at[k])
        send_cg(k, c).start()

    def a5(k):
        send_cg(k, 1 - c).wait_recv()
        ch, cl = split(cf[k].reshape(1024, 128))
        ph, pl_ = split(pv[k])
        mine = pv[k, :, pl.ds(pl.multiple_of(p * 128, 128), 128)]
        diag_out[k] = mine - dot3(ph, pl_, ch, cl)

    stages = (st0, st1, st2, st3, st4, st5, st6)

    def slot(t, carry):
        for o in range(5, -1, -1):
            tj = t - OFF[o]

            @pl.when((tj >= 0) & (tj % PACE == 0) & (tj < PACE * CHUNKS))
            def _(tj=tj, o=o):
                stages[o](tj // PACE)

        @pl.when(t == 0)
        def _():
            for k in range(2):
                for n in range(4):
                    send_u(k, n).start()
            prepare_grid()

        for k in range(2):
            @pl.when(t == UXH_AT[k])
            def _(k=k):
                take(r_u.at[k, 0], ub.at[k, pxh])
                for n in range(4, 7):
                    send_u(k, n).start()

        t6 = t - DONE

        @pl.when((t6 >= 0) & (t6 % PACE == 0) & (t6 < PACE * CHUNKS))
        def _():
            st6(t6 // PACE)

        for k in range(2):
            @pl.when(t == UPPER_AT[k])
            def _(k=k):
                prepare_upper(k)

        @pl.when(t == DONE)
        def _():
            locals_[19].wait()
            locals_[20].wait()

        for n, fn in enumerate((a0, a1, a2, a3, a4, a5)):
            for k in range(2):
                @pl.when(t == DONE + PACE * (4 * k + 3) + STAGES[n])
                def _(k=k, fn=fn):
                    fn(k)

        ts = t - SCHUR_LAG

        @pl.when((ts >= 0) & (ts % PACE == 0) & (ts < PACE * CHUNKS))
        def _():
            st_schur(ts // PACE)

        return carry

    lax.fori_loop(0, SLOTS, slot, 0)

    def drain(j, carry):
        left(s_own.at[j], lb.at[j, :, 0:7, 0, 0])
        left(s_a.at[j], lb.at[j, 0, 0:7, 0, 0])
        left(s_b.at[j], lb.at[j, 0, 0:7, 0, 0])
        left(s_c.at[j], lb.at[j, :, :, :, 0])
        left(s_x.at[j], two_blocks(j))
        return carry

    lax.fori_loop(0, CHUNKS, drain, 0)
    for k in range(2):
        left(s_u.at[k], ub.at[k, 0:7])
        left(s_p.at[k], rs.at[k])
    left(s_h, ss)
    left(s_cc, cr)
    left(s_z, zb)
    left(s_g, zb)
    left(s_cg, cr)


def body(trailing, anc_inverse, lower_panels, upper_panels_t, pivot_inverse, ancestors):
    dma = pltpu.SemaphoreType.DMA
    any_ = pl.BlockSpec(memory_space=pl.ANY)
    vmem = pl.BlockSpec(memory_space=pltpu.VMEM)
    arrivals = [(CHUNKS,), (CHUNKS, 4), (CHUNKS, 4), (CHUNKS,), (2, 2)] + [(2,)] * 6
    sems = [dma((CHUNKS,))] * 5 + [dma((2,))] * 2 + [dma] * 5 + [dma(shape) for shape in arrivals] + [dma((6,))]
    return pl.pallas_call(
        kernel,
        out_shape=(
            jax.ShapeDtypeStruct((1024, 256), F32),
            jax.ShapeDtypeStruct((2, 256, 128), F32),
            jax.ShapeDtypeStruct((2, 32, 128), F32),
        ),
        in_specs=[pl.BlockSpec(memory_space=pltpu.SMEM), any_, any_, any_, any_, any_],
        out_specs=(vmem, vmem, vmem),
        scratch_shapes=[
            pltpu.VMEM((CHUNKS, 2, Z, X, C, 32, 128), F32),
            pltpu.VMEM((CHUNKS, 1024, 256), BF16),
            pltpu.VMEM((CHUNKS, 1024, 256), BF16),
            pltpu.VMEM((1024, 256), F32),
            pltpu.VMEM((256, 1024), BF16),
            pltpu.VMEM((256, 1024), BF16),
            pltpu.VMEM((2, 8, 256, 128), F32),
            pltpu.VMEM((2, 8, 128, 256), BF16),
            pltpu.VMEM((2, 8, 128, 256), BF16),
            pltpu.VMEM((CHUNKS, 2, 256, 128), F32),
            pltpu.VMEM((2, 3, 2, 256, 128), F32),
            pltpu.VMEM((2, 256, 128), F32),
            pltpu.VMEM((2, 256, 128), F32),
            pltpu.VMEM((2, 2, 16, 32, 128), F32),
            pltpu.VMEM((2, 16, 32, 128), F32),
            pltpu.VMEM((2, 16, 32, 128), F32),
            pltpu.VMEM((2, 15, 32, 128), F32),
            pltpu.VMEM((2, 2, 16, 32, 128), F32),
            pltpu.VMEM((2, 32, 1024), F32),
            *sems,
        ],
        compiler_params=pltpu.CompilerParams(
            collective_id=0, has_side_effects=True, vmem_limit_bytes=56 * 1024 * 1024
        ),
    )(ancestors, trailing, anc_inverse, lower_panels, upper_panels_t, pivot_inverse)


def solution(mesh):
    in_specs = (
        P("prow", "pcol"),
        P("prow", "pcol"),
        P(None, ("prow", "pcol"), None),
        P(None, "pcol", "prow"),
        P(None, "pcol", None),
        P(),
    )
    out_specs = (P("prow", "pcol"), P(None, "pcol", "prow"), P(None, "pcol", "prow"))
    return jax.shard_map(body, mesh=mesh, in_specs=in_specs, out_specs=out_specs, check_vma=False)
```
